32 devices in a mesh: seq: 8 (over y, x, core), grp: 4 (over z).
Axes of the slice: x: 2, y: 2, z: 4, core: 2. Of those that a mesh axis runs over, the one named last changes fastest.
Arguments:
- tokens: bfloat16 [4, 8192, 3072], P('grp', 'seq'), may hold values from -24 to 24
- block_map: int32 [4, 64], P('grp', 'seq'), may hold values from 0 to 1, as said below
- slot_keys: bfloat16 [3072, 128], replicated, may hold values from -2 to 2
- gate_weight: bfloat16 [8, 3072, 4096], P('grp', None, 'seq'), may hold values from -0.109375 to 0.109375
- up_weight: bfloat16 [8, 3072, 4096], P('grp', None, 'seq'), may hold values from -0.109375 to 0.109375
- down_weight: bfloat16 [8, 4096, 3072], P('grp', 'seq'), may hold values from -0.09375 to 0.09375
Outputs:
- mixed: bfloat16 [4, 8192, 3072], P('grp', 'seq')
The draws below stay inside these ranges and needn't reach their ends.
Inputs may be any that keep to these rules, and one draw needn't show every extreme that they name: `block_map`: every sequence has at least one image block and at least one text block.
All inputs are finite; a program needn't handle non-finite values.
Results may differ from the reference program's by a relative error of at most 0.014.
Values may be sent and summed in bfloat16 or wider, within the bound.
No kernel may reach another device: no remote copies, remote signals or barrier semaphores. Data moves between devices by JAX's collectives and lax.ppermute only.
A program may use at most 128 MiB of HBM per device.

```python
import math
import jax
import jax.numpy as jnp
from jax import lax

D = 3072
FF = 4096
SPE = 16
BLOCK = 128
SEQS = 4
SEQ_LEN = 8192
EXPERTS = 8
SLOTS = 128
IMG_SLOTS = 96
NBLK = 64


def slot_table(key):
    values = jax.random.normal(jax.random.fold_in(key, 11), (D, SLOTS), jnp.float32)
    return jnp.clip(values, -4.0, 4.0) * (3.0 / math.sqrt(D))


def draw_slot_keys(key, part):
    return slot_table(key).astype(jnp.bfloat16)


def draw_tokens(key, part):
    base_key = jax.random.fold_in(key, 12)
    base = jnp.clip(jax.random.normal(base_key, (SEQS, SEQ_LEN, D), jnp.float32), -6.0, 6.0)
    return base.astype(jnp.bfloat16)


def draw_block_map(key, part):
    keys = jax.random.split(jax.random.fold_in(key, 21), 4)
    thresh = jax.random.randint(keys[0], (SEQS, 1), 1, 8)
    bits = (jax.random.randint(keys[1], (SEQS, NBLK), 0, 8) < thresh).astype(jnp.int32)
    first_pos = jax.random.randint(keys[2], (SEQS,), 0, NBLK)
    second_pos = (first_pos + 1 + jax.random.randint(keys[3], (SEQS,), 0, NBLK - 1)) % NBLK
    seq_index = jnp.arange(SEQS)
    bits = bits.at[seq_index, first_pos].set(0)
    bits = bits.at[seq_index, second_pos].set(1)
    return bits.astype(jnp.int32)


def levels(key, dims, shards, least, top_value):
    gain = 1.0
    for dim, shards_of in shards:
        steps = jax.random.uniform(jax.random.fold_in(jax.random.fold_in(key, 6), dim), (shards_of,), jnp.float32, least / len(shards), top_value / len(shards))
        gain = gain * jnp.repeat(jnp.exp(steps), dims[dim] // shards_of).reshape((-1,) + (1,) * (len(dims) - 1 - dim))
    return gain


def bell_draw(key, dims, deviation, reach, cuts=(), held_as=jnp.bfloat16):
    drawn = jax.random.normal(key, dims, jnp.float32) * deviation
    if len(cuts) > 0:
        drawn = levels(key, dims, cuts, -0.22, 0.18) * drawn
    return jnp.clip(drawn, min=-reach, max=reach).astype(held_as)


def setup_inputs(seed: int = 0) -> dict:
    splits = jax.random.split(jax.random.key(seed), 7)
    tokens = draw_tokens(jax.random.fold_in(splits[6], 71), 0)
    block_map = draw_block_map(jax.random.fold_in(splits[6], 71), 0)
    slot_keys = draw_slot_keys(jax.random.fold_in(splits[6], 71), 0)
    gate_weight = bell_draw(splits[3], (EXPERTS, D, FF), D ** -0.5, 0.109375, ((0, 4), (2, 8)))
    up_weight = bell_draw(splits[4], (EXPERTS, D, FF), D ** -0.5, 0.109375, ((0, 4), (2, 8)))
    down_weight = bell_draw(splits[5], (EXPERTS, FF, D), FF ** -0.5, 0.09375, ((0, 4), (1, 8)))
    return dict(tokens=tokens, block_map=block_map, slot_keys=slot_keys, gate_weight=gate_weight, up_weight=up_weight, down_weight=down_weight)


def allowed_table(seq_map):
    slot_text = (jnp.arange(SLOTS) >= IMG_SLOTS).astype(jnp.int32)
    token_mode = jnp.repeat(seq_map, BLOCK)
    return token_mode[:, None] == slot_text[None, :]

def reference(tokens, block_map, slot_keys, gate_weight, up_weight, down_weight):

    def slot_inputs(inputs):
        seq_tokens, seq_map = inputs
        allowed = allowed_table(seq_map)
        logits = jnp.dot(seq_tokens.astype(jnp.float32), slot_keys.astype(jnp.float32), preferred_element_type=jnp.float32)
        masked = jnp.where(allowed, logits, -1e+30)
        peak_value = jnp.max(masked, axis=0)
        weights = jnp.where(allowed, jnp.exp(masked - peak_value[None, :]), 0.0)
        totals = jnp.sum(weights, axis=0)
        slot_rows = jnp.dot(weights.astype(jnp.bfloat16).T.astype(jnp.float32), seq_tokens.astype(jnp.float32), preferred_element_type=jnp.float32)
        return (slot_rows / totals[:, None]).astype(jnp.bfloat16)
    slot_in = lax.map(slot_inputs, (tokens, block_map))
    by_expert = slot_in.reshape(SEQS, EXPERTS, SPE, D).transpose(1, 0, 2, 3).reshape(EXPERTS, SEQS * SPE, D)

    def expert(inputs):
        rows_in, w_gate, w_up, w_down = inputs
        gate_sum = jnp.dot(rows_in.astype(jnp.float32), w_gate.astype(jnp.float32), preferred_element_type=jnp.float32)
        up_sum = jnp.dot(rows_in.astype(jnp.float32), w_up.astype(jnp.float32), preferred_element_type=jnp.float32)
        hidden = (jax.nn.silu(gate_sum) * up_sum).astype(jnp.bfloat16)
        return jnp.dot(hidden.astype(jnp.float32), w_down.astype(jnp.float32), preferred_element_type=jnp.float32).astype(jnp.bfloat16)
    slot_out = lax.map(expert, (by_expert, gate_weight, up_weight, down_weight))
    slot_out = slot_out.reshape(EXPERTS, SEQS, SPE, D).transpose(1, 0, 2, 3).reshape(SEQS, SLOTS, D)

    def combine(inputs):
        seq_tokens, seq_map, seq_out = inputs
        allowed = allowed_table(seq_map)
        logits = jnp.dot(seq_tokens.astype(jnp.float32), slot_keys.astype(jnp.float32), preferred_element_type=jnp.float32)
        masked = jnp.where(allowed, logits, -1e+30)
        row_peak = jnp.max(masked, axis=1)
        scores = jnp.where(allowed, jnp.exp(masked - row_peak[:, None]), 0.0)
        mix_weights = (scores / jnp.sum(scores, axis=1)[:, None]).astype(jnp.bfloat16)
        return jnp.dot(mix_weights.astype(jnp.float32), seq_out.astype(jnp.float32), preferred_element_type=jnp.float32).astype(jnp.bfloat16)
    return lax.map(combine, (tokens, block_map, slot_out))
```

```python
import jax
import jax.numpy as jnp
from jax import lax
from jax.experimental import pallas as pl
from jax.experimental.pallas import tpu as pltpu
from jax.sharding import PartitionSpec as P

BLOCK = 128
LANES = 128
FLOOR = -1e30
F32 = jnp.float32
BF16 = jnp.bfloat16


def pack_stats(peak, total):
    rows = peak.shape[0]
    lane = lax.broadcasted_iota(jnp.int32, (rows, LANES), 1)
    block = jnp.zeros((rows, LANES), BF16).astype(F32)
    at = 0
    for value in (peak, total):
        rest = jnp.broadcast_to(value, (rows, LANES))
        for _ in range(3):
            part = rest.astype(BF16).astype(F32)
            block = jnp.where(lane == at, part, block)
            rest = rest - part
            at += 1
    return block.astype(BF16)


def unpack_stats(block):
    block = block.astype(F32)
    lane = lax.broadcasted_iota(jnp.int32, block.shape, 1)
    peak = jnp.sum(jnp.where(lane < 3, block, 0.0), axis=1, keepdims=True)
    total = jnp.sum(jnp.where((lane >= 3) & (lane < 6), block, 0.0), axis=1, keepdims=True)
    return peak, total


def merge(refs, rows, width):
    stats = [unpack_stats(ref[rows, width:]) for ref in refs]
    peak = stats[0][0]
    for other, _ in stats[1:]:
        peak = jnp.maximum(peak, other)
    scales = [jnp.exp(own - peak) for own, _ in stats]
    total = sum(s * t for s, (_, t) in zip(scales, stats))
    summed = sum(s * ref[rows, :width].astype(F32) for s, ref in zip(scales, refs))
    return peak, total, summed


def body_for(mesh):
    n_seq, n_grp = mesh.shape["seq"], mesh.shape["grp"]
    major = 1
    while major * major < n_seq:
        major *= 2
    minor = n_seq // major
    total_devices = n_seq * n_grp
    assert major * minor == n_seq and n_grp & (n_grp - 1) == 0

    def exchange(x, step, unit):
        pairs = []
        for i in range(total_devices):
            s, g = divmod(i, n_grp)
            if unit == "minor":
                s ^= step
            elif unit == "major":
                s ^= step * minor
            else:
                g ^= step
            pairs.append((i, s * n_grp + g))
        return lax.ppermute(x, ("seq", "grp"), pairs)

    def body(tokens, block_map, slot_keys, gate_weight, up_weight, down_weight):
        rows_here, width_all = tokens.shape[1:]
        slots = slot_keys.shape[1]
        blocks = block_map.shape[1]
        exp_dev, _, ff = gate_weight.shape
        width = width_all // minor
        wide = width + LANES
        piece = slots // major
        grain = piece // n_grp
        per_grp = slots // n_grp
        image_slots = 3 * slots // 4
        per_exp = major // exp_dev
        chunks = 4
        step_rows = rows_here // chunks
        blocks_in = blocks // chunks
        any_spec = pl.BlockSpec(memory_space=pl.ANY)
        vmem_spec = pl.BlockSpec(memory_space=pltpu.VMEM)
        smem_spec = pl.BlockSpec(memory_space=pltpu.SMEM)

        def place():
            s = lax.axis_index("seq")
            return s // minor, s % minor, lax.axis_index("grp")

        def shape(*dims):
            return jax.ShapeDtypeStruct(dims, BF16)

        def slot_ids(dims, dim):
            k, _, z = place()
            at = lax.broadcasted_iota(jnp.int32, dims, dim)
            p = at // piece
            q = (at % piece) // grain
            r = at % grain
            return (z ^ q) * per_grp + (k ^ p) * grain + r

        def column(off, size):
            return pl.ds(pl.multiple_of(off, LANES), size)

        def dispatch(tok_hbm, map_ref, keys_ref, *refs):
            outs = refs[:minor]
            mix_ref, tok, keys_p, logit, wt, sems = refs[minor:]
            k, m, z = place()
            copies = []
            for c in range(chunks):
                for h in range(minor):
                    cp = pltpu.make_async_copy(
                        tok_hbm.at[0, pl.ds(c * step_rows, step_rows), column((m ^ h) * width, width)],
                        tok.at[h, pl.ds(c * step_rows, step_rows), :],
                        sems.at[c, h],
                    )
                    cp.start()
                    copies.append(cp)
            wanted = slot_ids((slots, slots), 1)
            chosen = (lax.broadcasted_iota(jnp.int32, (slots, slots), 0) == wanted).astype(F32).astype(BF16)
            for h in range(minor):
                keys_p[h] = jnp.dot(
                    keys_ref[pl.ds((m ^ h) * width, width), :], chosen, preferred_element_type=F32
                ).astype(BF16)
            text = (slot_ids((1, slots), 1) >= image_slots).astype(jnp.int32)
            peak = jnp.full((1, slots), FLOOR, F32)
            for c in range(chunks):
                rows = slice(c * step_rows, (c + 1) * step_rows)
                value = None
                for h in range(minor):
                    copies[c * minor + h].wait()
                    part = jnp.dot(tok[h, rows, :], keys_p[h], preferred_element_type=F32)
                    value = part if value is None else value + part
                for b in range(blocks_in):
                    at = c * blocks_in + b
                    rows_b = slice(at * BLOCK, (at + 1) * BLOCK)
                    allowed = text == map_ref[0, at]
                    masked = jnp.where(allowed, value[b * BLOCK : (b + 1) * BLOCK], FLOOR)
                    logit[rows_b, :] = masked
                    peak = jnp.maximum(peak, jnp.max(masked, axis=0, keepdims=True))
                    row_peak = jnp.max(masked, axis=1, keepdims=True)
                    score = jnp.where(allowed, jnp.exp(masked - row_peak), 0.0)
                    mix_ref[rows_b, :] = (score / jnp.sum(score, axis=1, keepdims=True)).astype(BF16)
            total = jnp.zeros((1, slots), F32)
            for at in range(blocks):
                rows_b = slice(at * BLOCK, (at + 1) * BLOCK)
                allowed = text == map_ref[0, at]
                weight = jnp.where(allowed, jnp.exp(logit[rows_b, :] - peak), 0.0)
                total = total + jnp.sum(weight, axis=0, keepdims=True)
                wt[:, rows_b] = weight.T.astype(BF16)
            stats = pack_stats(
                jnp.broadcast_to(peak, (slots, slots)).T[:, :1],
                jnp.broadcast_to(total, (slots, slots)).T[:, :1],
            )
            for h in reversed(range(minor)):
                outs[h][:, width:] = stats
                outs[h][:, :width] = jnp.dot(wt[...], tok[h], preferred_element_type=F32).astype(BF16)

        *parts, mix = pl.pallas_call(
            dispatch,
            name="dispatch",
            in_specs=[any_spec, smem_spec, vmem_spec],
            out_specs=[vmem_spec] * (minor + 1),
            out_shape=[shape(slots, wide)] * minor + [shape(rows_here, slots)],
            scratch_shapes=[
                pltpu.VMEM((minor, rows_here, width), BF16),
                pltpu.VMEM((minor, width, slots), BF16),
                pltpu.VMEM((rows_here, slots), F32),
                pltpu.VMEM((slots, rows_here), BF16),
                pltpu.SemaphoreType.DMA((chunks, minor)),
            ],
        )(tokens, block_map, slot_keys)

        parts = [parts[0]] + [exchange(parts[h], h, "minor") for h in range(1, minor)]

        def merge_minor(*refs):
            ins, outs = refs[:minor], refs[minor:]
            for p in range(major):
                peak, total, summed = merge(ins, slice(p * piece, (p + 1) * piece), width)
                outs[p][:, :width] = summed.astype(BF16)
                outs[p][:, width:] = pack_stats(peak, total)

        parts = pl.pallas_call(
            merge_minor,
            name="merge_minor",
            in_specs=[vmem_spec] * minor,
            out_specs=[vmem_spec] * major,
            out_shape=[shape(piece, wide)] * major,
        )(*parts)

        parts = [parts[0]] + [exchange(parts[p], p, "major") for p in range(1, major)]

        def merge_major(*refs):
            ins, outs = refs[:major], refs[major:]
            _, total, summed = merge(ins, slice(None), width)
            value = summed / total
            for q in range(n_grp):
                outs[q][...] = value[q * grain : (q + 1) * grain].astype(BF16)

        parts = pl.pallas_call(
            merge_major,
            name="merge_major",
            in_specs=[vmem_spec] * major,
            out_specs=[vmem_spec] * n_grp,
            out_shape=[shape(grain, width)] * n_grp,
        )(*parts)

        def spread(parts):
            parts = [parts[0]] + [exchange(parts[q], q, "grp") for q in range(1, n_grp)]
            whole = jnp.concatenate(parts, axis=0)
            whole = [whole] + [exchange(whole, p, "major") for p in range(1, major)]
            return [whole] + [[exchange(x, h, "minor") for x in whole] for h in range(1, minor)]

        gathered = spread(parts)

        def experts(*refs):
            ins = refs[: minor * major]
            gate_hbm, up_hbm, down_hbm = refs[minor * major : minor * major + 3]
            outs = refs[minor * major + 3 : minor * major + 3 + minor]
            gate_v, up_v, down_v, sems = refs[minor * major + 3 + minor :]
            k, m, _ = place()
            copies = {}
            for t in range(exp_dev):
                e = (k // per_exp) ^ t
                for h in range(minor):
                    rows = pl.ds(pl.multiple_of((m ^ h) * width, LANES), width)
                    for i, (src, dst) in enumerate(((gate_hbm, gate_v), (up_hbm, up_v))):
                        cp = pltpu.make_async_copy(src.at[e, rows, :], dst.at[t, h], sems.at[i, t, h])
                        cp.start()
                        copies[i, t, h] = cp
                for h in range(minor):
                    cp = pltpu.make_async_copy(
                        down_hbm.at[e, :, column((m ^ h) * width, width)], down_v.at[t, h], sems.at[2, t, h]
                    )
                    cp.start()
                    copies[2, t, h] = cp
            for t in range(exp_dev):
                gate = up = None
                for h in range(minor):
                    x = jnp.concatenate(
                        [ins[h * major + p][...] for p in range(t * per_exp, (t + 1) * per_exp)], axis=0
                    )
                    copies[0, t, h].wait()
                    g = jnp.dot(x, gate_v[t, h], preferred_element_type=F32)
                    gate = g if gate is None else gate + g
                    copies[1, t, h].wait()
                    u = jnp.dot(x, up_v[t, h], preferred_element_type=F32)
                    up = u if up is None else up + u
                hidden = (gate / (1.0 + jnp.exp(-gate)) * up).astype(BF16)
                rows = slice(t * per_exp * piece, (t + 1) * per_exp * piece)
                for h in range(minor):
                    copies[2, t, h].wait()
                    outs[h][rows, :] = jnp.dot(hidden, down_v[t, h], preferred_element_type=F32).astype(BF16)

        parts = pl.pallas_call(
            experts,
            name="experts",
            in_specs=[vmem_spec] * (minor * major) + [any_spec] * 3,
            out_specs=[vmem_spec] * minor,
            out_shape=[shape(major * piece, width)] * minor,
            scratch_shapes=[
                pltpu.VMEM((exp_dev, minor, width, ff), BF16),
                pltpu.VMEM((exp_dev, minor, width, ff), BF16),
                pltpu.VMEM((exp_dev, minor, ff, width), BF16),
                pltpu.SemaphoreType.DMA((3, exp_dev, minor)),
            ],
        )(*[x for group in gathered for x in group], gate_weight, up_weight, down_weight)

        parts = [parts[0]] + [exchange(parts[h], h, "minor") for h in range(1, minor)]

        def add_minor(*refs):
            ins, outs = refs[:minor], refs[minor:]
            for p in range(major):
                rows = slice(p * piece, (p + 1) * piece)
                outs[p][...] = sum(ref[rows, :].astype(F32) for ref in ins).astype(BF16)

        parts = pl.pallas_call(
            add_minor,
            name="add_minor",
            in_specs=[vmem_spec] * minor,
            out_specs=[vmem_spec] * major,
            out_shape=[shape(piece, width)] * major,
        )(*parts)

        parts = [parts[0]] + [exchange(parts[p], p, "major") for p in range(1, major)]

        def add_major(*refs):
            ins, outs = refs[:major], refs[major:]
            value = sum(ref[...].astype(F32) for ref in ins)
            for q in range(n_grp):
                outs[q][...] = value[q * grain : (q + 1) * grain].astype(BF16)

        parts = pl.pallas_call(
            add_major,
            name="add_major",
            in_specs=[vmem_spec] * major,
            out_specs=[vmem_spec] * n_grp,
            out_shape=[shape(grain, width)] * n_grp,
        )(*parts)

        gathered = spread(parts)

        def combine(mix_ref, *refs):
            ins = refs[: minor * major]
            out_hbm, stage, sems = refs[minor * major :]
            _, m, _ = place()
            copies = []
            for c in range(chunks):
                rows = slice(c * step_rows, (c + 1) * step_rows)
                for h in range(minor):
                    value = jnp.concatenate([ins[h * major + p][...] for p in range(major)], axis=0)
                    stage[h, rows, :] = jnp.dot(
                        mix_ref[rows, :], value, preferred_element_type=F32
                    ).astype(BF16)
                    cp = pltpu.make_async_copy(
                        stage.at[h, rows, :],
                        out_hbm.at[0, rows, column((m ^ h) * width, width)],
                        sems.at[c, h],
                    )
                    cp.start()
                    copies.append(cp)
            for cp in copies:
                cp.wait()

        return pl.pallas_call(
            combine,
            name="combine",
            in_specs=[vmem_spec] * (1 + minor * major),
            out_specs=any_spec,
            out_shape=shape(1, rows_here, width_all),
            scratch_shapes=[
                pltpu.VMEM((minor, rows_here, width), BF16),
                pltpu.SemaphoreType.DMA((chunks, minor)),
            ],
        )(mix, *[x for group in gathered for x in group])

    return body


def solution(mesh):
    placed = (
        P("grp", "seq", None),
        P("grp", "seq"),
        P(),
        P("grp", None, "seq"),
        P("grp", None, "seq"),
        P("grp", "seq", None),
    )
    return jax.shard_map(
        body_for(mesh), mesh=mesh, in_specs=placed, out_specs=P("grp", "seq", None), check_vma=False
    )
```

```python
import jax
import jax.numpy as jnp
from jax import lax
from jax.experimental import pallas as pl
from jax.experimental.pallas import tpu as pltpu
from jax.sharding import PartitionSpec as P

BLOCK = 128
LANES = 128
FLOOR = -1e30
F32 = jnp.float32
BF16 = jnp.bfloat16


def pack_stats(peak, total):
    rows = peak.shape[0]
    lane = lax.broadcasted_iota(jnp.int32, (rows, LANES), 1)
    block = jnp.zeros((rows, LANES), BF16).astype(F32)
    at = 0
    for value in (peak, total):
        rest = jnp.broadcast_to(value, (rows, LANES))
        for _ in range(3):
            part = rest.astype(BF16).astype(F32)
            block = jnp.where(lane == at, part, block)
            rest = rest - part
            at += 1
    return block.astype(BF16)


def unpack_stats(block):
    block = block.astype(F32)
    lane = lax.broadcasted_iota(jnp.int32, block.shape, 1)
    peak = jnp.sum(jnp.where(lane < 3, block, 0.0), axis=1, keepdims=True)
    total = jnp.sum(jnp.where((lane >= 3) & (lane < 6), block, 0.0), axis=1, keepdims=True)
    return peak, total


def merge(refs, rows, width):
    stats = [unpack_stats(ref[rows, width:]) for ref in refs]
    peak = stats[0][0]
    for other, _ in stats[1:]:
        peak = jnp.maximum(peak, other)
    scales = [jnp.exp(own - peak) for own, _ in stats]
    total = sum(s * t for s, (_, t) in zip(scales, stats))
    summed = sum(s * ref[rows, :width].astype(F32) for s, ref in zip(scales, refs))
    return peak, total, summed


def body_for(mesh):
    n_seq, n_grp = mesh.shape["seq"], mesh.shape["grp"]
    major = 1
    while major * major < n_seq:
        major *= 2
    minor = n_seq // major
    total_devices = n_seq * n_grp
    assert major * minor == n_seq and n_grp & (n_grp - 1) == 0

    def exchange(x, step, unit):
        pairs = []
        for i in range(total_devices):
            s, g = divmod(i, n_grp)
            if unit == "minor":
                s ^= step
            elif unit == "major":
                s ^= step * minor
            else:
                g ^= step
            pairs.append((i, s * n_grp + g))
        return lax.ppermute(x, ("seq", "grp"), pairs)

    def body(tokens, block_map, slot_keys, gate_weight, up_weight, down_weight):
        rows_here, width_all = tokens.shape[1:]
        slots = slot_keys.shape[1]
        blocks = block_map.shape[1]
        exp_dev, _, ff = gate_weight.shape
        width = width_all // minor
        wide = width + LANES
        piece = slots // major
        grain = piece // n_grp
        per_grp = slots // n_grp
        image_slots = 3 * slots // 4
        per_exp = major // exp_dev
        chunks = 4
        step_rows = rows_here // chunks
        blocks_in = blocks // chunks
        any_spec = pl.BlockSpec(memory_space=pl.ANY)
        vmem_spec = pl.BlockSpec(memory_space=pltpu.VMEM)
        smem_spec = pl.BlockSpec(memory_space=pltpu.SMEM)

        def place():
            s = lax.axis_index("seq")
            return s // minor, s % minor, lax.axis_index("grp")

        def shape(*dims):
            return jax.ShapeDtypeStruct(dims, BF16)

        def near(*dims):
            return pltpu.VMEM(dims, BF16)

        def keep(xs):
            return [pltpu.with_memory_space_constraint(x, pltpu.VMEM) for x in xs]

        def slot_ids(dims, dim):
            k, _, z = place()
            at = lax.broadcasted_iota(jnp.int32, dims, dim)
            p = at // piece
            q = (at % piece) // grain
            r = at % grain
            return (z ^ q) * per_grp + (k ^ p) * grain + r

        def column(off, size):
            return pl.ds(pl.multiple_of(off, LANES), size)

        def dispatch(tok_hbm, map_ref, keys_ref, *refs):
            outs = refs[:minor]
            mix_ref, tok, keys_p, logit, wt, sems = refs[minor:]
            k, m, z = place()
            copies = []
            for c in range(chunks):
                for h in range(minor):
                    cp = pltpu.make_async_copy(
                        tok_hbm.at[0, pl.ds(c * step_rows, step_rows), column((m ^ h) * width, width)],
                        tok.at[h, pl.ds(c * step_rows, step_rows), :],
                        sems.at[c, h],
                    )
                    cp.start()
                    copies.append(cp)
            wanted = slot_ids((slots, slots), 1)
            chosen = (lax.broadcasted_iota(jnp.int32, (slots, slots), 0) == wanted).astype(F32).astype(BF16)
            for h in range(minor):
                keys_p[h] = jnp.dot(
                    keys_ref[pl.ds((m ^ h) * width, width), :], chosen, preferred_element_type=F32
                ).astype(BF16)
            text = (slot_ids((1, slots), 1) >= image_slots).astype(jnp.int32)
            peak = jnp.full((1, slots), FLOOR, F32)
            for c in range(chunks):
                rows = slice(c * step_rows, (c + 1) * step_rows)
                value = None
                for h in range(minor):
                    copies[c * minor + h].wait()
                    part = jnp.dot(tok[h, rows, :], keys_p[h], preferred_element_type=F32)
                    value = part if value is None else value + part
                for b in range(blocks_in):
                    at = c * blocks_in + b
                    rows_b = slice(at * BLOCK, (at + 1) * BLOCK)
                    allowed = text == map_ref[0, at]
                    masked = jnp.where(allowed, value[b * BLOCK : (b + 1) * BLOCK], FLOOR)
                    logit[rows_b, :] = masked
                    peak = jnp.maximum(peak, jnp.max(masked, axis=0, keepdims=True))
                    row_peak = jnp.max(masked, axis=1, keepdims=True)
                    score = jnp.where(allowed, jnp.exp(masked - row_peak), 0.0)
                    mix_ref[rows_b, :] = (score / jnp.sum(score, axis=1, keepdims=True)).astype(BF16)
            total = jnp.zeros((1, slots), F32)
            for at in range(blocks):
                rows_b = slice(at * BLOCK, (at + 1) * BLOCK)
                allowed = text == map_ref[0, at]
                weight = jnp.where(allowed, jnp.exp(logit[rows_b, :] - peak), 0.0)
                total = total + jnp.sum(weight, axis=0, keepdims=True)
                wt[:, rows_b] = weight.T.astype(BF16)
            stats = pack_stats(
                jnp.broadcast_to(peak, (slots, slots)).T[:, :1],
                jnp.broadcast_to(total, (slots, slots)).T[:, :1],
            )
            for h in reversed(range(minor)):
                outs[h][:, width:] = stats
                outs[h][:, :width] = jnp.dot(wt[...], tok[h], preferred_element_type=F32).astype(BF16)

        *parts, mix = pl.pallas_call(
            dispatch,
            name="dispatch",
            in_specs=[any_spec, smem_spec, vmem_spec],
            out_specs=[vmem_spec] * (minor + 1),
            out_shape=[near(slots, wide)] * minor + [near(rows_here, slots)],
            scratch_shapes=[
                pltpu.VMEM((minor, rows_here, width), BF16),
                pltpu.VMEM((minor, width, slots), BF16),
                pltpu.VMEM((rows_here, slots), F32),
                pltpu.VMEM((slots, rows_here), BF16),
                pltpu.SemaphoreType.DMA((chunks, minor)),
            ],
        )(tokens, block_map, slot_keys)

        parts = [parts[0]] + [exchange(parts[h], h, "minor") for h in range(1, minor)]

        def merge_minor(*refs):
            ins, outs = refs[:minor], refs[minor:]
            for p in range(major):
                peak, total, summed = merge(ins, slice(p * piece, (p + 1) * piece), width)
                outs[p][:, :width] = summed.astype(BF16)
                outs[p][:, width:] = pack_stats(peak, total)

        parts = pl.pallas_call(
            merge_minor,
            name="merge_minor",
            in_specs=[vmem_spec] * minor,
            out_specs=[vmem_spec] * major,
            out_shape=[near(piece, wide)] * major,
        )(*keep(parts))

        parts = [parts[0]] + [exchange(parts[p], p, "major") for p in range(1, major)]

        def merge_major(*refs):
            ins, outs = refs[:major], refs[major:]
            _, total, summed = merge(ins, slice(None), width)
            value = summed / total
            for q in range(n_grp):
                outs[q][...] = value[q * grain : (q + 1) * grain].astype(BF16)

        parts = pl.pallas_call(
            merge_major,
            name="merge_major",
            in_specs=[vmem_spec] * major,
            out_specs=[vmem_spec] * n_grp,
            out_shape=[near(grain, width)] * n_grp,
        )(*keep(parts))

        def spread(parts):
            parts = [parts[0]] + [exchange(parts[q], q, "grp") for q in range(1, n_grp)]
            whole = jnp.concatenate(parts, axis=0)
            whole = [whole] + [exchange(whole, p, "major") for p in range(1, major)]
            return [whole] + [[exchange(x, h, "minor") for x in whole] for h in range(1, minor)]

        gathered = spread(parts)

        def experts(*refs):
            ins = refs[: minor * major]
            gate_hbm, up_hbm, down_hbm = refs[minor * major : minor * major + 3]
            outs = refs[minor * major + 3 : minor * major + 3 + minor]
            gate_v, up_v, down_v, sems = refs[minor * major + 3 + minor :]
            k, m, _ = place()
            copies = {}
            for t in range(exp_dev):
                e = (k // per_exp) ^ t
                for h in range(minor):
                    rows = pl.ds(pl.multiple_of((m ^ h) * width, LANES), width)
                    for i, (src, dst) in enumerate(((gate_hbm, gate_v), (up_hbm, up_v))):
                        cp = pltpu.make_async_copy(src.at[e, rows, :], dst.at[t, h], sems.at[i, t, h])
                        cp.start()
                        copies[i, t, h] = cp
                for h in range(minor):
                    cp = pltpu.make_async_copy(
                        down_hbm.at[e, :, column((m ^ h) * width, width)], down_v.at[t, h], sems.at[2, t, h]
                    )
                    cp.start()
                    copies[2, t, h] = cp
            for t in range(exp_dev):
                gate = up = None
                for h in range(minor):
                    x = jnp.concatenate(
                        [ins[h * major + p][...] for p in range(t * per_exp, (t + 1) * per_exp)], axis=0
                    )
                    copies[0, t, h].wait()
                    g = jnp.dot(x, gate_v[t, h], preferred_element_type=F32)
                    gate = g if gate is None else gate + g
                    copies[1, t, h].wait()
                    u = jnp.dot(x, up_v[t, h], preferred_element_type=F32)
                    up = u if up is None else up + u
                hidden = (gate / (1.0 + jnp.exp(-gate)) * up).astype(BF16)
                rows = slice(t * per_exp * piece, (t + 1) * per_exp * piece)
                for h in range(minor):
                    copies[2, t, h].wait()
                    outs[h][rows, :] = jnp.dot(hidden, down_v[t, h], preferred_element_type=F32).astype(BF16)

        parts = pl.pallas_call(
            experts,
            name="experts",
            in_specs=[vmem_spec] * (minor * major) + [any_spec] * 3,
            out_specs=[vmem_spec] * minor,
            out_shape=[near(major * piece, width)] * minor,
            scratch_shapes=[
                pltpu.VMEM((exp_dev, minor, width, ff), BF16),
                pltpu.VMEM((exp_dev, minor, width, ff), BF16),
                pltpu.VMEM((exp_dev, minor, ff, width), BF16),
                pltpu.SemaphoreType.DMA((3, exp_dev, minor)),
            ],
        )(*keep([x for group in gathered for x in group]), gate_weight, up_weight, down_weight)

        parts = [parts[0]] + [exchange(parts[h], h, "minor") for h in range(1, minor)]

        def add_minor(*refs):
            ins, outs = refs[:minor], refs[minor:]
            for p in range(major):
                rows = slice(p * piece, (p + 1) * piece)
                outs[p][...] = sum(ref[rows, :].astype(F32) for ref in ins).astype(BF16)

        parts = pl.pallas_call(
            add_minor,
            name="add_minor",
            in_specs=[vmem_spec] * minor,
            out_specs=[vmem_spec] * major,
            out_shape=[near(piece, width)] * major,
        )(*keep(parts))

        parts = [parts[0]] + [exchange(parts[p], p, "major") for p in range(1, major)]

        def add_major(*refs):
            ins, outs = refs[:major], refs[major:]
            value = sum(ref[...].astype(F32) for ref in ins)
            for q in range(n_grp):
                outs[q][...] = value[q * grain : (q + 1) * grain].astype(BF16)

        parts = pl.pallas_call(
            add_major,
            name="add_major",
            in_specs=[vmem_spec] * major,
            out_specs=[vmem_spec] * n_grp,
            out_shape=[near(grain, width)] * n_grp,
        )(*keep(parts))

        gathered = spread(parts)

        def combine(mix_ref, *refs):
            ins = refs[: minor * major]
            out_hbm, stage, sems = refs[minor * major :]
            _, m, _ = place()
            copies = []
            for c in range(chunks):
                rows = slice(c * step_rows, (c + 1) * step_rows)
                for h in range(minor):
                    value = jnp.concatenate([ins[h * major + p][...] for p in range(major)], axis=0)
                    stage[h, rows, :] = jnp.dot(
                        mix_ref[rows, :], value, preferred_element_type=F32
                    ).astype(BF16)
                    cp = pltpu.make_async_copy(
                        stage.at[h, rows, :],
                        out_hbm.at[0, rows, column((m ^ h) * width, width)],
                        sems.at[c, h],
                    )
                    cp.start()
                    copies.append(cp)
            for cp in copies:
                cp.wait()

        return pl.pallas_call(
            combine,
            name="combine",
            in_specs=[vmem_spec] * (1 + minor * major),
            out_specs=any_spec,
            out_shape=shape(1, rows_here, width_all),
            scratch_shapes=[
                pltpu.VMEM((minor, rows_here, width), BF16),
                pltpu.SemaphoreType.DMA((chunks, minor)),
            ],
        )(*keep([mix] + [x for group in gathered for x in group]))

    return body


def solution(mesh):
    placed = (
        P("grp", "seq", None),
        P("grp", "seq"),
        P(),
        P("grp", None, "seq"),
        P("grp", None, "seq"),
        P("grp", "seq", None),
    )
    return jax.shard_map(
        body_for(mesh), mesh=mesh, in_specs=placed, out_specs=P("grp", "seq", None), check_vma=False
    )
```
